256 devices in a mesh: dp: 8 (over z), seq: 32 (over x, y, core).
Axes of the slice: x: 4, y: 4, z: 8, core: 2. Of those that a mesh axis runs over, the one named last changes fastest.
Arguments:
- question: bfloat16 [2048, 3584], P(('dp', 'seq')), parts along dimension 0, may hold values from -6 to 6
- block_ids: int32 [256, 64], P(('dp', 'seq')), parts along dimension 0, may hold values from -1 to 255, as said below
- block_counts: int32 [256], P(('dp', 'seq')), parts along dimension 0, may hold values from 1 to 64
- cache_keys: bfloat16 [262144, 512], P(('dp', 'seq')), parts along dimension 0, may hold values from -4 to 4
- cache_values: bfloat16 [262144, 512], P(('dp', 'seq')), parts along dimension 0, may hold values from -6 to 6
- frame_query: bfloat16 [65536, 3584], P(('dp', 'seq')), parts along dimension 0, may hold values from -6 to 6
- frame_keys: bfloat16 [65536, 512], P(('dp', 'seq')), parts along dimension 0, may hold values from -4 to 4
- frame_values: bfloat16 [65536, 512], P(('dp', 'seq')), parts along dimension 0, may hold values from -6 to 6
- frame_reach: int32 [65536], P(('dp', 'seq')), parts along dimension 0, may hold values from 1 to 128
Outputs:
- answer: bfloat16 [2048, 3584], P(('dp', 'seq')), parts along dimension 0
- frame_out: bfloat16 [65536, 3584], P(('dp', 'seq')), parts along dimension 0
The draws below stay inside these ranges and needn't reach their ends.
There are 8 independent parts, one for each index of `dp`. The reference program is written for one: setup_inputs(seed, part) draws one part's arguments, and reference() takes and returns one part's arrays. A program takes and returns all parts, laid end to end along the dimension named above; each array names one. Nothing has to cross between parts.
Inputs may be any that keep to these rules, and one draw needn't show every extreme that they name: `block_ids`: row t's first block_counts[t] entries are distinct blocks; every later entry is -1. Block b lies in the cache rows held by seq index b // 8. At most 2 of one tile's blocks lie on one seq index, and some tile takes 2 blocks from every index.
All inputs are finite; a program needn't handle non-finite values.
Results may differ from the reference program's by a relative error of at most 0.017.
Values may be sent and summed in bfloat16 or wider, within the bound.
A program may use at most 128 MiB of HBM per device.

```python
import jax
import jax.numpy as jnp
from jax import lax

HEADS = 28
KV_HEADS = 4
HEAD_DIM = 128
GROUP = 7
BLOCK = 128
PER_OWNER = 2
WIN = 128
BLK_DEV = 8
QT_DEV = 8
TILES = 32
MAXB = 64
NBLK = 256
CACHE = 32768
QTOK = 256
FTOK = 8192


def drawn_rows(key, row_count, row_width):
    values = jax.random.normal(key, (row_count, row_width), jnp.float32)
    return jnp.clip(values, -4.0, 4.0)


def draw_question(key, part):
    inner_key = jax.random.fold_in(key, 11)
    return drawn_rows(inner_key, QTOK, HEADS * HEAD_DIM).astype(jnp.bfloat16)


def draw_cache_keys(key, part):
    inner_key = jax.random.fold_in(key, 12)
    return drawn_rows(inner_key, CACHE, KV_HEADS * HEAD_DIM).astype(jnp.bfloat16)


def draw_frame_query(key, part):
    inner_key = jax.random.fold_in(key, 13)
    return drawn_rows(inner_key, FTOK, HEADS * HEAD_DIM).astype(jnp.bfloat16)


def draw_frame_keys(key, part):
    inner_key = jax.random.fold_in(key, 14)
    return drawn_rows(inner_key, FTOK, KV_HEADS * HEAD_DIM).astype(jnp.bfloat16)


def retrieval(key):
    inner_key = jax.random.fold_in(key, 4242)
    owners = jnp.arange(TILES, dtype=jnp.int32)
    hotness = jax.random.randint(jax.random.fold_in(inner_key, 1), (TILES,), 1, 4)
    rolled = jax.random.randint(jax.random.fold_in(inner_key, 2), (TILES, TILES), 0, PER_OWNER + 1)
    taken_count = jnp.clip(rolled + hotness[None, :] - 3, 0, PER_OWNER)
    anchor = jax.random.randint(jax.random.fold_in(inner_key, 3), (TILES,), 0, TILES)
    taken_count = jnp.maximum(taken_count, (owners[None, :] == anchor[:, None]).astype(jnp.int32))
    fullest = jax.random.randint(jax.random.fold_in(inner_key, 4), (), 0, TILES)
    taken_count = jnp.where((owners == fullest)[:, None], PER_OWNER, taken_count).astype(jnp.int32)
    order_keys = jax.random.randint(jax.random.fold_in(inner_key, 5), (TILES, TILES, BLK_DEV), 0, 1048576) * BLK_DEV + jnp.arange(BLK_DEV, dtype=jnp.int32)
    chosen = jnp.argsort(order_keys, axis=-1)[..., :PER_OWNER].astype(jnp.int32)
    slot_index = jnp.arange(PER_OWNER, dtype=jnp.int32)
    listing = jnp.where(slot_index[None, None, :] < taken_count[..., None], owners[None, :, None] * BLK_DEV + chosen, -1)
    listing = listing.reshape(TILES, MAXB).astype(jnp.int32)
    is_valid = listing >= 0
    column_index = jnp.arange(MAXB, dtype=jnp.int32)
    mixing = jax.random.randint(jax.random.fold_in(inner_key, 6), (TILES, MAXB), 0, 1048576) * MAXB + column_index
    mixing = jnp.where(is_valid, mixing, 1048576 * MAXB + column_index)
    new_order = jnp.argsort(mixing, axis=-1)
    listing = jnp.take_along_axis(listing, new_order, axis=-1)
    return (listing, jnp.sum(taken_count, axis=-1).astype(jnp.int32))


def draw_block_ids(key, part):
    listing, counted = retrieval(key)
    return listing


def draw_block_counts(key, part):
    listing, counted = retrieval(key)
    return counted


def place_ends(entries, stream_key, low, high):
    spot = [jax.random.randint(jax.random.fold_in(stream_key, axis), (), 0, length) for axis, length in enumerate(entries.shape)]
    widest = entries.shape.index(max(entries.shape))
    next_to = spot[:widest] + [(spot[widest] + 1) % entries.shape[widest]] + spot[widest + 1:]
    return entries.at[tuple(spot)].set(low).at[tuple(next_to)].set(high)


def steps_of(key, shape, cuts, low, high):
    level, own = 1.0, jax.random.fold_in(key, 6)
    for axis_at, shards_of in cuts:
        steps = jnp.exp(jax.random.uniform(jax.random.fold_in(own, axis_at), (shards_of,), jnp.float32, low / len(cuts), high / len(cuts)))
        level = level * jnp.repeat(steps, shape[axis_at] // shards_of).reshape([-1 if axis == axis_at else 1 for axis in range(len(shape))])
    return level


def scatter_about(key, extent, spread, reach, cuts=(), kind=jnp.bfloat16):
    entries = spread * jax.random.normal(key, extent, jnp.float32)
    if cuts:
        entries = entries * steps_of(key, extent, cuts, -0.22, 0.18)
    return jnp.clip(entries, -reach, reach).astype(kind)


def setup_inputs(seed: int = 0, part: int = 0) -> dict:
    seeds = jax.random.split(jax.random.key(seed), 10)
    own_keys = jax.random.split(jax.random.fold_in(seeds[9], part), 10)
    question = draw_question(jax.random.fold_in(jax.random.fold_in(seeds[9], part), 71), part)
    block_ids = draw_block_ids(jax.random.fold_in(jax.random.fold_in(seeds[9], part), 71), part)
    block_counts = draw_block_counts(jax.random.fold_in(jax.random.fold_in(seeds[9], part), 71), part)
    cache_keys = draw_cache_keys(jax.random.fold_in(jax.random.fold_in(seeds[9], part), 71), part)
    cache_values = scatter_about(own_keys[4], (CACHE, KV_HEADS * HEAD_DIM), 1.0, 6.0, ((0, 32),))
    frame_query = draw_frame_query(jax.random.fold_in(jax.random.fold_in(seeds[9], part), 71), part)
    frame_keys = draw_frame_keys(jax.random.fold_in(jax.random.fold_in(seeds[9], part), 71), part)
    frame_values = scatter_about(own_keys[7], (FTOK, KV_HEADS * HEAD_DIM), 1.0, 6.0, ((0, 32),))
    frame_reach = place_ends(jax.random.randint(own_keys[8], (FTOK,), 1, WIN + 1), jax.random.fold_in(own_keys[8], 1), 1, WIN).astype(jnp.int32)
    return {"question": question, "block_ids": block_ids, "block_counts": block_counts, "cache_keys": cache_keys, "cache_values": cache_values, "frame_query": frame_query, "frame_keys": frame_keys, "frame_values": frame_values, "frame_reach": frame_reach}


NEGATIVE = -1e30


def attention(queries, keys_flat, values_flat, allowed):
    row_count = queries.shape[0]
    grouped = queries.astype(jnp.float32).reshape(row_count, KV_HEADS, GROUP, HEAD_DIM)
    key_heads = keys_flat.astype(jnp.float32).reshape(-1, KV_HEADS, HEAD_DIM)
    value_heads = values_flat.astype(jnp.float32).reshape(-1, KV_HEADS, HEAD_DIM)
    outputs = []
    for kv_head in range(KV_HEADS):
        scores = jnp.einsum("rgd,kd->rgk", grouped[:, kv_head], key_heads[:, kv_head], precision=lax.Precision.HIGHEST) * (HEAD_DIM ** -0.5)
        scores = jnp.where(allowed[:, None, :], scores, NEGATIVE)
        highest = jnp.max(scores, axis=-1, keepdims=True)
        weights = jnp.exp(scores - highest)
        totals = jnp.sum(weights, axis=-1, keepdims=True)
        rounded = lax.optimization_barrier(weights.astype(jnp.bfloat16)).astype(jnp.float32)
        mixed_sum = jnp.einsum("rgk,kd->rgd", rounded, value_heads[:, kv_head], precision=lax.Precision.HIGHEST)
        outputs.append(mixed_sum / totals)
    return jnp.stack(outputs, 1).reshape(row_count, HEADS * HEAD_DIM).astype(jnp.bfloat16)


def reference(question, block_ids, block_counts, cache_keys, cache_values, frame_query, frame_keys, frame_values, frame_reach):
    def one_tile(inputs):
        tile_queries, listing, count_here = inputs
        usable = (jnp.arange(MAXB, dtype=jnp.int32) < count_here) & (listing >= 0)
        chosen = jnp.any((listing[:, None] == jnp.arange(NBLK, dtype=jnp.int32)[None, :]) & usable[:, None], axis=0)
        key_ok = jnp.broadcast_to(chosen[:, None], (NBLK, BLOCK)).reshape(CACHE)
        return attention(tile_queries, cache_keys, cache_values, jnp.broadcast_to(key_ok[None, :], (QT_DEV, CACHE)))

    answer = lax.map(one_tile, (question.reshape(TILES, QT_DEV, HEADS * HEAD_DIM), block_ids, block_counts))
    answer = answer.reshape(QTOK, HEADS * HEAD_DIM)

    key_pad = jnp.concatenate([jnp.zeros((WIN, KV_HEADS * HEAD_DIM), frame_keys.dtype), frame_keys], 0)
    value_pad = jnp.concatenate([jnp.zeros((WIN, KV_HEADS * HEAD_DIM), frame_values.dtype), frame_values], 0)

    def one_block(block_index):
        first_row = (block_index * WIN).astype(jnp.int32)
        block_queries = lax.dynamic_slice_in_dim(frame_query, first_row, WIN, 0)
        block_keys = lax.dynamic_slice_in_dim(key_pad, first_row, 2 * WIN, 0)
        block_values = lax.dynamic_slice_in_dim(value_pad, first_row, 2 * WIN, 0)
        reach_rows = lax.dynamic_slice_in_dim(frame_reach, first_row, WIN, 0)
        query_pos = first_row + jnp.arange(WIN, dtype=jnp.int32)
        key_pos = first_row - WIN + jnp.arange(2 * WIN, dtype=jnp.int32)
        allowed = (key_pos[None, :] <= query_pos[:, None]) & (key_pos[None, :] > (query_pos - reach_rows)[:, None]) & (key_pos >= 0)[None, :]
        return attention(block_queries, block_keys, block_values, allowed)

    frame_out = lax.map(one_block, jnp.arange(FTOK // WIN, dtype=jnp.int32)).reshape(FTOK, HEADS * HEAD_DIM)
    return answer, frame_out
```

```python
import functools
import math

import jax
import jax.numpy as jnp
from jax import lax
from jax.experimental import pallas as pl
from jax.experimental.pallas import tpu as pltpu
from jax.sharding import PartitionSpec as P

HEADS = 28
KV_HEADS = 4
HEAD_DIM = 128
GROUP = 7
BLOCK = 128
WIN = 128
BLK_DEV = 8
NEGATIVE = -1e30
EXP2_SCALE = HEAD_DIM ** (-0.5) * math.log2(math.e)


def dot_t(a, b):
    return lax.dot_general(a, b, (((1,), (1,)), ((), ())), preferred_element_type=jnp.float32)


def frame_kernel(q_ref, k_ref, v_ref, ek_ref, ev_ref, reach_ref, o_ref):
    myself = lax.axis_index("seq")
    block = pl.program_id(0)
    row = lax.broadcasted_iota(jnp.int32, (WIN, WIN), 0)
    col = lax.broadcasted_iota(jnp.int32, (WIN, WIN), 1)
    current = col <= row
    distance = jnp.where(current, row - col, row - col + WIN)
    reach = jnp.transpose(jnp.broadcast_to(reach_ref[pl.ds(block, 1), :], (WIN, WIN)))
    at_start = (block == 0) & (myself == 0)
    allowed = (distance < reach) & (current | jnp.logical_not(at_start))
    bias = jnp.where(allowed, 0.0, NEGATIVE)
    own = jnp.where(current, 1.0, 0.0).astype(jnp.bfloat16)
    before = jnp.where(current, 0.0, 1.0).astype(jnp.bfloat16)
    first = block == 0
    keys_own = k_ref[pl.ds(block * WIN, WIN), :]
    values_own = v_ref[pl.ds(block * WIN, WIN), :]
    keys_before = jnp.where(first, ek_ref[...], k_ref[0:WIN, :])
    values_before = jnp.where(first, ev_ref[...], v_ref[0:WIN, :])
    keys = jnp.concatenate([keys_before, keys_own], 0)
    ones = jnp.ones((2 * WIN, HEAD_DIM), jnp.bfloat16)
    values = jnp.concatenate([jnp.concatenate([values_before, values_own], 0), ones], 1)
    for g in range(GROUP):
        lanes = slice(g * HEAD_DIM, (g + 1) * HEAD_DIM)
        both = dot_t(q_ref[:, lanes], keys)
        scores = jnp.where(current, both[:, WIN:], both[:, :WIN]) + bias
        highest = jnp.max(scores, axis=1, keepdims=True)
        weights = jnp.exp2((scores - highest) * EXP2_SCALE).astype(jnp.bfloat16)
        split = jnp.concatenate([weights * before, weights * own], 1)
        mixed = jnp.dot(split, values, preferred_element_type=jnp.float32)
        o_ref[:, lanes] = (mixed[:, :HEAD_DIM] / mixed[:, HEAD_DIM:]).astype(jnp.bfloat16)


def frame_attention(frame_query, frame_keys, frame_values, edge_keys, edge_values, reach):
    rows = frame_query.shape[0]
    width = GROUP * HEAD_DIM
    return pl.pallas_call(
        frame_kernel,
        grid=(rows // WIN, KV_HEADS),
        in_specs=[
            pl.BlockSpec((WIN, width), lambda i, g: (i, g)),
            pl.BlockSpec((rows, HEAD_DIM), lambda i, g: (0, g)),
            pl.BlockSpec((rows, HEAD_DIM), lambda i, g: (0, g)),
            pl.BlockSpec((WIN, HEAD_DIM), lambda i, g: (0, g)),
            pl.BlockSpec((WIN, HEAD_DIM), lambda i, g: (0, g)),
            pl.BlockSpec((rows // WIN, WIN), lambda i, g: (0, 0)),
        ],
        out_specs=pl.BlockSpec((WIN, width), lambda i, g: (i, g)),
        out_shape=jax.ShapeDtypeStruct(frame_query.shape, jnp.bfloat16),
    )(frame_query, frame_keys, frame_values, edge_keys, edge_values, reach.reshape(rows // WIN, WIN))


def tile_partial(q, keys_two, values_two, bias, emit):
    stat = jnp.zeros((8, HEAD_DIM), jnp.float32)
    lane = lax.broadcasted_iota(jnp.int32, (8, HEAD_DIM), 1)
    ones = jnp.ones((2 * BLOCK, HEAD_DIM), jnp.bfloat16)
    rows = GROUP * 8
    scores = []
    for pair in range(2):
        base = pair * 2 * rows
        for half in range(2):
            kv = pair * 2 + half
            lanes = slice(kv * HEAD_DIM, (kv + 1) * HEAD_DIM)
            if half == 0:
                s = dot_t(q[base : base + 64], keys_two[:, lanes])[:rows]
            else:
                s = dot_t(q[base + 48 : base + 112], keys_two[:, lanes])[8:]
            scores.append(s + bias)
    highs = [jnp.max(s, axis=1, keepdims=True) for s in scores]
    weights = [jnp.exp2((s - h) * EXP2_SCALE) for s, h in zip(scores, highs)]
    for pair in range(2):
        w = jnp.concatenate(weights[pair * 2 : pair * 2 + 2], 0).astype(jnp.bfloat16)
        outs = []
        for half in range(2):
            kv = pair * 2 + half
            lanes = slice(kv * HEAD_DIM, (kv + 1) * HEAD_DIM)
            v = jnp.concatenate([values_two[:, lanes], ones], 1)
            if half == 0:
                o = jnp.dot(w[0:64], v, preferred_element_type=jnp.float32)[:rows]
            else:
                o = jnp.dot(w[48:112], v, preferred_element_type=jnp.float32)[8:]
            outs.append(o[:, :HEAD_DIM])
            for g in range(GROUP):
                head = kv * GROUP + g
                part = slice(g * 8, g * 8 + 8)
                stat = jnp.where(lane == head, highs[kv][part], stat)
                stat = jnp.where(lane == head + 32, o[part, HEAD_DIM:], stat)
        emit(pair * 2 * rows, jnp.concatenate(outs, 0).astype(jnp.bfloat16))
    return stat


def question_kernel(pick_ref, q_ref, k_ref, v_ref, o_ref, s_ref):
    col = lax.broadcasted_iota(jnp.int32, (1, 2 * BLOCK), 1)

    def step(t, carry):
        low = pick_ref[t, 0]
        high = pick_ref[t, 1]
        low_ok = low < BLK_DEV
        high_ok = (high >= 0) & (high != low)
        at_low = pl.multiple_of(jnp.minimum(low, BLK_DEV - 1) * BLOCK, BLOCK)
        at_high = pl.multiple_of(jnp.maximum(high, 0) * BLOCK, BLOCK)
        keys_two = jnp.concatenate([k_ref[pl.ds(at_low, BLOCK), :], k_ref[pl.ds(at_high, BLOCK), :]], 0)
        values_two = jnp.concatenate([v_ref[pl.ds(at_low, BLOCK), :], v_ref[pl.ds(at_high, BLOCK), :]], 0)
        bias_low = jnp.where(low_ok, 0.0, NEGATIVE)
        bias_high = jnp.where(high_ok, 0.0, NEGATIVE)
        bias = jnp.where(col < BLOCK, bias_low, bias_high)

        def emit(at, value):
            o_ref[t, at : at + value.shape[0], :] = value

        s_ref[t] = tile_partial(q_ref[t], keys_two, values_two, bias, emit)
        return carry

    lax.fori_loop(0, q_ref.shape[0], step, 0)


def combine_kernel(o_ref, s_ref, a_ref):
    stats = s_ref[...]
    highest = jnp.max(stats, axis=0)
    scale = jnp.exp2((stats - highest[None]) * EXP2_SCALE)
    tiles = stats.shape[0]
    total = jnp.zeros_like(highest)
    for i in range(tiles):
        total = total + scale[i] * pltpu.roll(stats[i], HEAD_DIM - 32, 1)
    share = scale / total[None]
    for head in range(HEADS):
        mixed = jnp.zeros((8, HEAD_DIM), jnp.float32)
        for i in range(tiles):
            mixed = mixed + share[i][:, head : head + 1] * o_ref[i, head * 8 : head * 8 + 8, :].astype(jnp.float32)
        a_ref[:, head * HEAD_DIM : (head + 1) * HEAD_DIM] = mixed.astype(jnp.bfloat16)


def per_device(
    question, block_ids, block_counts, cache_keys, cache_values, frame_query, frame_keys, frame_values, frame_reach
):
    devices = lax.axis_size("seq")
    myself = lax.axis_index("seq")
    frame_rows = frame_query.shape[0]
    pairs = [(s, (s + 1) % devices) for s in range(devices)]
    edge_keys, edge_values = lax.ppermute(
        (frame_keys[frame_rows - WIN :], frame_values[frame_rows - WIN :]), "seq", pairs
    )
    columns = jnp.arange(block_ids.shape[1], dtype=jnp.int32)
    own_ids = jnp.where(columns[None, :] < block_counts[:, None], block_ids, -1)
    lists = lax.all_gather(own_ids, "seq", axis=0, tiled=True)
    tiles = lists.shape[0]
    local = jnp.where((lists >= 0) & (lists // BLK_DEV == myself), lists % BLK_DEV, -1)
    high = jnp.max(local, axis=1)
    low = jnp.min(jnp.where(local >= 0, local, BLK_DEV), axis=1)
    picks = jnp.stack([low, high], 1)
    rows = question.shape[0]
    heads_first = question.reshape(rows, HEADS, HEAD_DIM).transpose(1, 0, 2).reshape(1, rows * HEADS, HEAD_DIM)
    questions = lax.all_gather(heads_first, "seq", axis=0, tiled=True)
    whole = pl.BlockSpec(memory_space=pltpu.VMEM)
    partial, stats = pl.pallas_call(
        question_kernel,
        in_specs=[pl.BlockSpec(memory_space=pltpu.SMEM), whole, whole, whole],
        out_specs=(whole, whole),
        out_shape=(
            jax.ShapeDtypeStruct(questions.shape, jnp.bfloat16),
            jax.ShapeDtypeStruct((tiles, 8, HEAD_DIM), jnp.float32),
        ),
    )(picks, questions, cache_keys, cache_values)
    frame_out = frame_attention(frame_query, frame_keys, frame_values, edge_keys, edge_values, frame_reach)
    partial = lax.all_to_all(partial, "seq", split_axis=0, concat_axis=0, tiled=True)
    stats = lax.all_to_all(stats, "seq", split_axis=0, concat_axis=0, tiled=True)
    answer = pl.pallas_call(
        combine_kernel,
        in_specs=[whole, whole],
        out_specs=whole,
        out_shape=jax.ShapeDtypeStruct(question.shape, jnp.bfloat16),
    )(partial, stats)
    return answer, frame_out


def solution(mesh):
    flat = P(("dp", "seq"))
    wide = P(("dp", "seq"), None)
    return jax.shard_map(
        per_device,
        mesh=mesh,
        in_specs=(wide, wide, flat, wide, wide, wide, wide, wide, flat),
        out_specs=(wide, wide),
        check_vma=False,
    )
```

```python
import functools
import math

import jax
import jax.numpy as jnp
from jax import lax
from jax.experimental import pallas as pl
from jax.experimental.pallas import tpu as pltpu
from jax.sharding import PartitionSpec as P

HEADS = 28
KV_HEADS = 4
HEAD_DIM = 128
GROUP = 7
BLOCK = 128
WIN = 128
BLK_DEV = 8
NEGATIVE = -1e30
EXP2_SCALE = HEAD_DIM ** (-0.5) * math.log2(math.e)


def dot_t(a, b):
    return lax.dot_general(a, b, (((1,), (1,)), ((), ())), preferred_element_type=jnp.float32)


def frame_block(block, first_index, fq, fo, fk, fv, reach_ref):
    row = lax.broadcasted_iota(jnp.int32, (WIN, WIN), 0)
    col = lax.broadcasted_iota(jnp.int32, (WIN, WIN), 1)
    current = col <= row
    distance = jnp.where(current, row - col, row - col + WIN)
    reach = jnp.transpose(jnp.broadcast_to(reach_ref[block : block + 1, :], (WIN, WIN)))
    allowed = distance < reach
    if block == 0:
        allowed = allowed & (current | jnp.logical_not(first_index))
    bias = jnp.where(allowed, 0.0, NEGATIVE)
    own = jnp.where(current, 1.0, 0.0).astype(jnp.bfloat16)
    before = jnp.where(current, 0.0, 1.0).astype(jnp.bfloat16)
    ones = jnp.ones((2 * WIN, HEAD_DIM), jnp.bfloat16)
    rows = slice(block * WIN, (block + 1) * WIN)
    window = slice(block * WIN, (block + 2) * WIN)

    def step(kv, carry):
        at = pl.ds(pl.multiple_of(kv * HEAD_DIM, HEAD_DIM), HEAD_DIM)
        keys = fk[window, at]
        values = jnp.concatenate([fv[window, at], ones], 1)
        for g in range(GROUP):
            lanes = pl.ds(pl.multiple_of((kv * GROUP + g) * HEAD_DIM, HEAD_DIM), HEAD_DIM)
            both = dot_t(fq[rows, lanes], keys)
            scores = jnp.where(current, both[:, WIN:], both[:, :WIN]) + bias
            highest = jnp.max(scores, axis=1, keepdims=True)
            weights = jnp.exp2((scores - highest) * EXP2_SCALE).astype(jnp.bfloat16)
            split = jnp.concatenate([weights * before, weights * own], 1)
            mixed = jnp.dot(split, values, preferred_element_type=jnp.float32)
            fo[rows, lanes] = (mixed[:, :HEAD_DIM] / mixed[:, HEAD_DIM:]).astype(jnp.bfloat16)
        return carry

    lax.fori_loop(0, KV_HEADS, step, 0)


def tile_partial(q, keys, values, bias):
    stat = jnp.zeros((8, HEAD_DIM), jnp.float32)
    lane = lax.broadcasted_iota(jnp.int32, (8, HEAD_DIM), 1)
    ones = jnp.ones((keys.shape[0], HEAD_DIM), jnp.bfloat16)
    rows = GROUP * 8
    first, second = slice(0, HEAD_DIM), slice(HEAD_DIM, 2 * HEAD_DIM)
    scores = [
        dot_t(q[0:64], keys[:, first])[:rows] + bias,
        dot_t(q[48:112], keys[:, second])[8:] + bias,
    ]
    highs = [jnp.max(s, axis=1, keepdims=True) for s in scores]
    weights = [jnp.exp2((s - h) * EXP2_SCALE) for s, h in zip(scores, highs)]
    w = jnp.concatenate(weights, 0).astype(jnp.bfloat16)
    outs = [
        jnp.dot(w[0:64], jnp.concatenate([values[:, first], ones], 1), preferred_element_type=jnp.float32)[:rows],
        jnp.dot(w[48:112], jnp.concatenate([values[:, second], ones], 1), preferred_element_type=jnp.float32)[8:],
    ]
    for kv in range(2):
        for g in range(GROUP):
            head = kv * GROUP + g
            part = slice(g * 8, g * 8 + 8)
            stat = jnp.where(lane == head, highs[kv][part], stat)
            stat = jnp.where(lane == head + 32, outs[kv][part, HEAD_DIM:], stat)
    return jnp.concatenate([o[:, :HEAD_DIM] for o in outs], 0).astype(jnp.bfloat16), stat


def kernel(
    devices,
    picks_ref, q_ref, reach_ref, ck_ref, cv_ref, fq_ref, fk_ref, fv_ref,
    a_ref, fo_ref,
    kk, vv, fq, fo, fk, fv, q_all, picks_all, picks_s, ob, sb, og, sg,
    local, swap_send, swap_recv, q_send, q_recv, p_send, p_recv, o_send, o_recv, s_send, s_recv,
):
    me = lax.axis_index("seq")
    core = lax.rem(me, 2)
    other = 1 - core
    partner = me + 1 - 2 * core
    after = lax.rem(me + 1, devices)
    half = 2 * HEAD_DIM
    rows = fq.shape[0]

    def here(src, dst, i):
        return pltpu.make_async_copy(src, dst, local.at[i])

    def there(src, dst, send, recv, device):
        return pltpu.make_async_remote_copy(
            src_ref=src, dst_ref=dst, send_sem=send, recv_sem=recv,
            device_id={"seq": device}, device_id_type=pl.DeviceIdType.MESH,
        )

    mine = pl.ds(pl.multiple_of(core * half, half), half)
    theirs = pl.ds(pl.multiple_of(other * half, half), half)
    loads = [
        here(fq_ref, fq, 0),
        here(fk_ref, fk.at[pl.ds(WIN, rows)], 1),
        here(fv_ref, fv.at[pl.ds(WIN, rows)], 2),
        here(ck_ref.at[:, :, mine], kk.at[core], 3),
        here(cv_ref.at[:, :, mine], vv.at[core], 4),
        here(q_ref.at[core], q_all.at[me], 5),
        here(picks_ref, picks_all.at[me], 6),
    ]
    for load in loads:
        load.start()

    barrier = pltpu.get_barrier_semaphore()

    def greet(i, carry):
        pl.semaphore_signal(
            barrier, inc=1, device_id={"seq": lax.rem(me + i, devices)}, device_id_type=pl.DeviceIdType.MESH
        )
        return carry

    lax.fori_loop(1, devices, greet, 0)
    pl.semaphore_wait(barrier, devices - 1)

    edges = [
        there(fk_ref.at[pl.ds(rows - WIN, WIN)], fk.at[pl.ds(0, WIN)], swap_send.at[0], swap_recv.at[0], after),
        there(fv_ref.at[pl.ds(rows - WIN, WIN)], fv.at[pl.ds(0, WIN)], swap_send.at[1], swap_recv.at[1], after),
    ]
    swaps = [
        there(ck_ref.at[:, :, theirs], kk.at[core], swap_send.at[2], swap_recv.at[2], partner),
        there(cv_ref.at[:, :, theirs], vv.at[core], swap_send.at[3], swap_recv.at[3], partner),
    ]
    swaps_in = [
        there(ck_ref.at[:, :, theirs], kk.at[other], swap_send.at[2], swap_recv.at[2], partner),
        there(cv_ref.at[:, :, theirs], vv.at[other], swap_send.at[3], swap_recv.at[3], partner),
    ]
    for copy in edges:
        copy.start()

    def question_to(t, slot):
        return there(q_ref.at[lax.rem(t, 2)], q_all.at[slot], q_send.at[t], q_recv.at[slot], t)

    def picks_to(t, slot):
        return there(picks_ref, picks_all.at[slot], p_send.at[t], p_recv.at[slot], t)

    def partial_to(t, slot):
        return there(ob.at[t], og.at[slot], o_send.at[t], o_recv.at[slot], t)

    def stat_to(t, slot):
        return there(sb.at[t], sg.at[slot], s_send.at[t], s_recv.at[slot], t)

    def send_questions(i, carry):
        t = lax.rem(me + i, devices)
        picks_to(t, me).start()
        question_to(t, me).start()
        return carry

    lax.fori_loop(1, devices, send_questions, 0)
    for copy in swaps:
        copy.start()

    for load in loads[:3]:
        load.wait()
    frame_block(1, me == 0, fq, fo, fk, fv, reach_ref)
    for copy in edges:
        copy.wait_recv()
    frame_block(0, me == 0, fq, fo, fk, fv, reach_ref)
    late = here(fo.at[pl.ds(WIN, WIN)], fo_ref.at[pl.ds(WIN, WIN)], 0)
    late.start()

    for load in loads[3:]:
        load.wait()

    def got_picks(i, carry):
        t = lax.rem(me + devices - i, devices)
        picks_to(t, t).wait_recv()
        return carry

    lax.fori_loop(1, devices, got_picks, 0)
    to_scalars = here(picks_all, picks_s, 7)
    to_scalars.start()
    for copy in swaps_in:
        copy.wait_recv()
    to_scalars.wait()

    chip = me - core
    block_of = lax.broadcasted_iota(jnp.int32, (1, 4 * BLOCK), 1) // BLOCK

    def step(i, carry):
        t = lax.rem(me + devices - i, devices)

        @pl.when(i > 0)
        def _():
            question_to(t, t).wait_recv()

        keys, values = [], []
        bias = jnp.zeros((1, 4 * BLOCK), jnp.float32)
        for c in range(2):
            low = picks_s[t, 0, chip + c]
            high = picks_s[t, 0, devices + chip + c]
            usable = (low < BLK_DEV, (high >= 0) & (high != low))
            index = (jnp.minimum(low, BLK_DEV - 1), jnp.maximum(high, 0))
            for j in range(2):
                keys.append(kk[c, index[j]])
                values.append(vv[c, index[j]])
                bias = jnp.where(block_of == 2 * c + j, jnp.where(usable[j], 0.0, NEGATIVE), bias)
        o, stat = tile_partial(q_all[t], jnp.concatenate(keys, 0), jnp.concatenate(values, 0), bias)
        ob[t] = o
        sb[t] = stat

        @pl.when(i > 1)
        def _():
            previous = lax.rem(t + 1, devices)
            partial_to(previous, me).start()
            stat_to(previous, me).start()

        return carry

    lax.fori_loop(0, devices, step, 0)
    partial_to(after, me).start()
    stat_to(after, me).start()
    keep = [here(ob.at[me], og.at[me], 1), here(sb.at[me], sg.at[me], 2)]
    for copy in keep:
        copy.start()
    early = here(fo.at[pl.ds(0, WIN)], fo_ref.at[pl.ds(0, WIN)], 3)
    early.start()

    def sent(i, carry):
        t = lax.rem(me + i, devices)
        question_to(t, me).wait_send()
        picks_to(t, me).wait_send()
        return carry

    lax.fori_loop(1, devices, sent, 0)
    for copy in edges + swaps:
        copy.wait_send()
    for copy in keep:
        copy.wait()

    def arrived(i, carry):
        t = lax.rem(me + i, devices)
        partial_to(t, t).wait_recv()
        stat_to(t, t).wait_recv()
        return carry

    lax.fori_loop(1, devices, arrived, 0)

    for h in range(2):
        stats = [sg[2 * c + h] for c in range(devices // 2)]
        highest = stats[0]
        for s in stats[1:]:
            highest = jnp.maximum(highest, s)
        scales = [jnp.exp2((s - highest) * EXP2_SCALE) for s in stats]
        total = jnp.zeros_like(highest)
        for s, scale in zip(stats, scales):
            total = total + scale * pltpu.roll(s, HEAD_DIM - 32, 1)
        shares = [scale / total for scale in scales]
        for head in range(HEADS // 2):
            mixed = jnp.zeros((8, HEAD_DIM), jnp.float32)
            for c in range(devices // 2):
                part = og[2 * c + h, head * 8 : head * 8 + 8, :].astype(jnp.float32)
                mixed = mixed + shares[c][:, head : head + 1] * part
            whole = h * (HEADS // 2) + head
            a_ref[:, whole * HEAD_DIM : (whole + 1) * HEAD_DIM] = mixed.astype(jnp.bfloat16)

    def done(i, carry):
        t = lax.rem(me + i, devices)
        partial_to(t, me).wait_send()
        stat_to(t, me).wait_send()
        return carry

    lax.fori_loop(1, devices, done, 0)
    late.wait()
    early.wait()


def per_device(
    question, block_ids, block_counts, cache_keys, cache_values, frame_query, frame_keys, frame_values, frame_reach
):
    devices = lax.axis_size("seq")
    rows = question.shape[0]
    frame_rows, width = frame_query.shape
    kv_width = cache_keys.shape[1]
    columns = jnp.arange(block_ids.shape[1], dtype=jnp.int32)
    ids = jnp.where(columns < block_counts[0], block_ids[0], -1)
    holders = jnp.arange(devices, dtype=jnp.int32)
    held = (ids[None, :] >= 0) & (ids[None, :] // BLK_DEV == holders[:, None])
    low = jnp.min(jnp.where(held, ids[None, :] % BLK_DEV, BLK_DEV), axis=1)
    high = jnp.max(jnp.where(held, ids[None, :] % BLK_DEV, -1), axis=1)
    picks = jnp.pad(jnp.concatenate([low, high]), (0, HEAD_DIM - 2 * devices)).reshape(1, HEAD_DIM)
    half_rows = rows * HEADS // 2
    halves = question.reshape(rows, HEADS, HEAD_DIM).transpose(1, 0, 2).reshape(2, half_rows, HEAD_DIM)
    vmem = pl.BlockSpec(memory_space=pltpu.VMEM)
    anywhere = pl.BlockSpec(memory_space=pl.ANY)
    sems = pltpu.SemaphoreType.DMA((devices,))
    bf16 = jnp.bfloat16
    return pl.pallas_call(
        functools.partial(kernel, devices),
        in_specs=[vmem, vmem, vmem] + [anywhere] * 5,
        out_specs=(vmem, anywhere),
        out_shape=(
            jax.ShapeDtypeStruct(question.shape, bf16),
            jax.ShapeDtypeStruct(frame_query.shape, bf16),
        ),
        scratch_shapes=[
            pltpu.VMEM((2, BLK_DEV, BLOCK, kv_width // 2), bf16),
            pltpu.VMEM((2, BLK_DEV, BLOCK, kv_width // 2), bf16),
            pltpu.VMEM((frame_rows, width), bf16),
            pltpu.VMEM((frame_rows, width), bf16),
            pltpu.VMEM((WIN + frame_rows, kv_width), bf16),
            pltpu.VMEM((WIN + frame_rows, kv_width), bf16),
            pltpu.VMEM((devices, half_rows, HEAD_DIM), bf16),
            pltpu.VMEM((devices, 1, HEAD_DIM), jnp.int32),
            pltpu.SMEM((devices, 1, HEAD_DIM), jnp.int32),
            pltpu.VMEM((devices, half_rows, HEAD_DIM), bf16),
            pltpu.VMEM((devices, 8, HEAD_DIM), jnp.float32),
            pltpu.VMEM((devices, half_rows, HEAD_DIM), bf16),
            pltpu.VMEM((devices, 8, HEAD_DIM), jnp.float32),
            pltpu.SemaphoreType.DMA((8,)),
            pltpu.SemaphoreType.DMA((4,)),
            pltpu.SemaphoreType.DMA((4,)),
            sems, sems, sems, sems, sems, sems, sems, sems,
        ],
        compiler_params=pltpu.CompilerParams(collective_id=0, has_side_effects=True),
    )(
        picks, halves, frame_reach.reshape(frame_rows // WIN, WIN), cache_keys.reshape(BLK_DEV, BLOCK, kv_width),
        cache_values.reshape(BLK_DEV, BLOCK, kv_width), frame_query, frame_keys, frame_values,
    )


def solution(mesh):
    flat = P(("dp", "seq"))
    wide = P(("dp", "seq"), None)
    return jax.shard_map(
        per_device,
        mesh=mesh,
        in_specs=(wide, wide, flat, wide, wide, wide, wide, wide, flat),
        out_specs=(wide, wide),
        check_vma=False,
    )
```

```python
import functools
import math

import jax
import jax.numpy as jnp
from jax import lax
from jax.experimental import pallas as pl
from jax.experimental.pallas import tpu as pltpu
from jax.sharding import PartitionSpec as P

HEADS = 28
KV_HEADS = 4
HEAD_DIM = 128
GROUP = 7
BLOCK = 128
WIN = 128
BLK_DEV = 8
TOGETHER = 2
NEGATIVE = -1e30
EXP2_SCALE = HEAD_DIM ** (-0.5) * math.log2(math.e)


def dot_t(a, b):
    return lax.dot_general(a, b, (((1,), (1,)), ((), ())), preferred_element_type=jnp.float32)


def frame_block(block, first_index, fq, fo, fk, fv, reach_ref):
    row = lax.broadcasted_iota(jnp.int32, (WIN, WIN), 0)
    col = lax.broadcasted_iota(jnp.int32, (WIN, WIN), 1)
    current = col <= row
    distance = jnp.where(current, row - col, row - col + WIN)
    reach = jnp.transpose(jnp.broadcast_to(reach_ref[block : block + 1, :], (WIN, WIN)))
    allowed = distance < reach
    if block == 0:
        allowed = allowed & (current | jnp.logical_not(first_index))
    bias = jnp.where(allowed, 0.0, NEGATIVE)
    own = jnp.where(current, 1.0, 0.0).astype(jnp.bfloat16)
    before = jnp.where(current, 0.0, 1.0).astype(jnp.bfloat16)
    ones = jnp.ones((2 * WIN, HEAD_DIM), jnp.bfloat16)
    rows = slice(block * WIN, (block + 1) * WIN)
    window = slice(block * WIN, (block + 2) * WIN)

    def step(kv, carry):
        at = pl.ds(pl.multiple_of(kv * HEAD_DIM, HEAD_DIM), HEAD_DIM)
        keys = fk[window, at]
        values = jnp.concatenate([fv[window, at], ones], 1)
        for g in range(GROUP):
            lanes = pl.ds(pl.multiple_of((kv * GROUP + g) * HEAD_DIM, HEAD_DIM), HEAD_DIM)
            both = dot_t(fq[rows, lanes], keys)
            scores = jnp.where(current, both[:, WIN:], both[:, :WIN]) + bias
            highest = jnp.max(scores, axis=1, keepdims=True)
            weights = jnp.exp2((scores - highest) * EXP2_SCALE).astype(jnp.bfloat16)
            split = jnp.concatenate([weights * before, weights * own], 1)
            mixed = jnp.dot(split, values, preferred_element_type=jnp.float32)
            fo[rows, lanes] = (mixed[:, :HEAD_DIM] / mixed[:, HEAD_DIM:]).astype(jnp.bfloat16)
        return carry

    lax.fori_loop(0, KV_HEADS, step, 0)


def tile_partial(q, keys, values, bias):
    stat = jnp.zeros((8, HEAD_DIM), jnp.float32)
    lane = lax.broadcasted_iota(jnp.int32, (8, HEAD_DIM), 1)
    rows = GROUP * 8
    head_row = lax.broadcasted_iota(jnp.int32, (2 * rows, HEAD_DIM), 0)
    upper = jnp.where(head_row < rows, 1.0, 0.0).astype(jnp.bfloat16)
    lower = jnp.where(head_row < rows, 0.0, 1.0).astype(jnp.bfloat16)
    scores = dot_t(jnp.concatenate([q * upper, q * lower], 1), keys) + bias
    highest = jnp.max(scores, axis=1, keepdims=True)
    weights = jnp.exp2((scores - highest) * EXP2_SCALE)
    total = jnp.sum(weights, axis=1, keepdims=True)
    mixed = jnp.dot(weights.astype(jnp.bfloat16), values, preferred_element_type=jnp.float32)
    for head in range(2 * GROUP):
        part = slice(head * 8, head * 8 + 8)
        stat = jnp.where(lane == head, highest[part], stat)
        stat = jnp.where(lane == head + 32, total[part], stat)
    return jnp.where(head_row < rows, mixed[:, :HEAD_DIM], mixed[:, HEAD_DIM:]).astype(jnp.bfloat16), stat


def pick_row(ids_ref, count_ref, devices):
    width = ids_ref.shape[1]
    ids = jnp.concatenate([ids_ref[...], jnp.full((1, HEAD_DIM - width), -1, jnp.int32)], 1)
    ids = jnp.transpose(jnp.broadcast_to(ids, (HEAD_DIM, HEAD_DIM)))
    slot = lax.broadcasted_iota(jnp.int32, ids.shape, 0)
    lane = lax.broadcasted_iota(jnp.int32, ids.shape, 1)
    holder = jnp.where(lane < devices, lane, lane - devices)
    held = (slot < count_ref[...]) & (ids >= 0) & ((ids >> 3) == holder)
    low = jnp.min(jnp.where(held, ids & (BLK_DEV - 1), BLK_DEV), axis=0, keepdims=True)
    high = jnp.max(jnp.where(held, ids & (BLK_DEV - 1), -1), axis=0, keepdims=True)
    return jnp.where(lane[:1] < devices, low, high)


def kernel(
    devices,
    ids_ref, count_ref, question_ref, reach_ref, ck_ref, cv_ref, fq_ref, fk_ref, fv_ref,
    a_ref, fo_ref,
    picks_ref, q_ref, kk, vv, fq, fo, fk, fv, q_all, picks_all, picks_s, ob, sb, og, sg,
    local, swap_send, swap_recv, q_send, q_recv, p_send, p_recv, o_send, o_recv, s_send, s_recv,
):
    me = lax.axis_index("seq")
    core = lax.rem(me, 2)
    other = 1 - core
    partner = me + 1 - 2 * core
    after = lax.rem(me + 1, devices)
    half = 2 * HEAD_DIM
    rows = fq.shape[0]

    def here(src, dst, i):
        return pltpu.make_async_copy(src, dst, local.at[i])

    def there(src, dst, send, recv, device):
        return pltpu.make_async_remote_copy(
            src_ref=src, dst_ref=dst, send_sem=send, recv_sem=recv,
            device_id={"seq": device}, device_id_type=pl.DeviceIdType.MESH,
        )

    mine = pl.ds(pl.multiple_of(core * half, half), half)
    theirs = pl.ds(pl.multiple_of(other * half, half), half)
    loads = [
        here(fq_ref, fq, 0),
        here(fk_ref, fk.at[pl.ds(WIN, rows)], 1),
        here(fv_ref, fv.at[pl.ds(WIN, rows)], 2),
        here(ck_ref.at[:, :, mine], kk.at[core], 3),
        here(cv_ref.at[:, :, mine], vv.at[core], 4),
    ]
    for load in loads:
        load.start()

    barrier = pltpu.get_barrier_semaphore()

    def greet(i, carry):
        pl.semaphore_signal(
            barrier, inc=1, device_id={"seq": lax.rem(me + i, devices)}, device_id_type=pl.DeviceIdType.MESH
        )
        return carry

    lax.fori_loop(1, devices, greet, 0)
    picks_ref[...] = pick_row(ids_ref, count_ref, devices)
    for head in range(HEADS):
        at = head % (HEADS // 2) * 8
        q_ref[head // (HEADS // 2), at : at + 8, :] = question_ref[:, head * HEAD_DIM : (head + 1) * HEAD_DIM]
    pl.semaphore_wait(barrier, devices - 1)

    edges = [
        there(fk_ref.at[pl.ds(rows - WIN, WIN)], fk.at[pl.ds(0, WIN)], swap_send.at[0], swap_recv.at[0], after),
        there(fv_ref.at[pl.ds(rows - WIN, WIN)], fv.at[pl.ds(0, WIN)], swap_send.at[1], swap_recv.at[1], after),
    ]
    swaps = [
        there(ck_ref.at[:, :, theirs], kk.at[core], swap_send.at[2], swap_recv.at[2], partner),
        there(cv_ref.at[:, :, theirs], vv.at[core], swap_send.at[3], swap_recv.at[3], partner),
    ]
    swaps_in = [
        there(ck_ref.at[:, :, theirs], kk.at[other], swap_send.at[2], swap_recv.at[2], partner),
        there(cv_ref.at[:, :, theirs], vv.at[other], swap_send.at[3], swap_recv.at[3], partner),
    ]
    own = [here(q_ref.at[core], q_all.at[me], 5), here(picks_ref, picks_all.at[me], 6)]
    for copy in edges + own:
        copy.start()

    def question_to(t, slot):
        return there(q_ref.at[lax.rem(t, 2)], q_all.at[slot], q_send.at[t], q_recv.at[slot], t)

    def picks_to(t, slot):
        return there(picks_ref, picks_all.at[slot], p_send.at[t], p_recv.at[slot], t)

    def partial_to(t, slot):
        return there(ob.at[t], og.at[slot], o_send.at[t], o_recv.at[slot], t)

    def stat_to(t, slot):
        return there(sb.at[t], sg.at[slot], s_send.at[t], s_recv.at[slot], t)

    def send_questions(i, carry):
        t = lax.rem(me + i, devices)
        picks_to(t, me).start()
        question_to(t, me).start()
        return carry

    lax.fori_loop(1, devices, send_questions, 0)
    for copy in swaps:
        copy.start()

    for load in loads[:3]:
        load.wait()
    frame_block(1, me == 0, fq, fo, fk, fv, reach_ref)
    for copy in edges:
        copy.wait_recv()
    frame_block(0, me == 0, fq, fo, fk, fv, reach_ref)
    late = here(fo.at[pl.ds(WIN, WIN)], fo_ref.at[pl.ds(WIN, WIN)], 0)
    late.start()

    for load in loads[3:] + own:
        load.wait()

    def got_picks(i, carry):
        t = lax.rem(me + devices - i, devices)
        picks_to(t, t).wait_recv()
        return carry

    lax.fori_loop(1, devices, got_picks, 0)
    to_scalars = here(picks_all, picks_s, 7)
    to_scalars.start()
    for copy in swaps_in:
        copy.wait_recv()
    to_scalars.wait()

    chip = me - core
    block_of = lax.broadcasted_iota(jnp.int32, (1, 4 * BLOCK), 1) // BLOCK

    def gathered(t):
        keys, values = [], []
        bias = jnp.zeros((1, 4 * BLOCK), jnp.float32)
        for c in range(2):
            low = picks_s[t, 0, chip + c]
            high = picks_s[t, 0, devices + chip + c]
            usable = (low < BLK_DEV, (high >= 0) & (high != low))
            index = (jnp.minimum(low, BLK_DEV - 1), jnp.maximum(high, 0))
            for j in range(2):
                keys.append(kk[c, index[j]])
                values.append(vv[c, index[j]])
                bias = jnp.where(block_of == 2 * c + j, jnp.where(usable[j], 0.0, NEGATIVE), bias)
        return jnp.concatenate(keys, 0), jnp.concatenate(values, 0), bias

    def tile_of(i):
        return lax.rem(me + devices - i, devices)

    def step(j, carry):
        first = j * TOGETHER
        for u in range(TOGETHER):
            if u:
                question_to(tile_of(first + u), tile_of(first + u)).wait_recv()
            else:

                @pl.when(j > 0)
                def _():
                    question_to(tile_of(first), tile_of(first)).wait_recv()

        results = [tile_partial(q_all[tile_of(first + u)], *gathered(tile_of(first + u))) for u in range(TOGETHER)]
        for u in range(TOGETHER):
            ob[tile_of(first + u)], sb[tile_of(first + u)] = results[u]
        for u in range(TOGETHER):

            @pl.when(first - TOGETHER + u > 0)
            def _():
                partial_to(tile_of(first - TOGETHER + u), me).start()
                stat_to(tile_of(first - TOGETHER + u), me).start()

        return carry

    lax.fori_loop(0, devices // TOGETHER, step, 0)
    for u in range(TOGETHER):
        partial_to(tile_of(devices - TOGETHER + u), me).start()
        stat_to(tile_of(devices - TOGETHER + u), me).start()
    keep = [here(ob.at[me], og.at[me], 1), here(sb.at[me], sg.at[me], 2)]
    for copy in keep:
        copy.start()
    early = here(fo.at[pl.ds(0, WIN)], fo_ref.at[pl.ds(0, WIN)], 3)
    early.start()

    def sent(i, carry):
        t = lax.rem(me + i, devices)
        question_to(t, me).wait_send()
        picks_to(t, me).wait_send()
        return carry

    lax.fori_loop(1, devices, sent, 0)
    for copy in edges + swaps:
        copy.wait_send()
    for copy in keep:
        copy.wait()

    def arrived(i, carry):
        t = lax.rem(me + i, devices)
        partial_to(t, t).wait_recv()
        stat_to(t, t).wait_recv()
        return carry

    lax.fori_loop(1, devices, arrived, 0)

    for h in range(2):
        stats = [sg[2 * c + h] for c in range(devices // 2)]
        highest = stats[0]
        for s in stats[1:]:
            highest = jnp.maximum(highest, s)
        scales = [jnp.exp2((s - highest) * EXP2_SCALE) for s in stats]
        total = jnp.zeros_like(highest)
        for s, scale in zip(stats, scales):
            total = total + scale * pltpu.roll(s, HEAD_DIM - 32, 1)
        shares = [scale / total for scale in scales]
        for head in range(HEADS // 2):
            mixed = jnp.zeros((8, HEAD_DIM), jnp.float32)
            for c in range(devices // 2):
                part = og[2 * c + h, head * 8 : head * 8 + 8, :].astype(jnp.float32)
                mixed = mixed + shares[c][:, head : head + 1] * part
            whole = h * (HEADS // 2) + head
            a_ref[:, whole * HEAD_DIM : (whole + 1) * HEAD_DIM] = mixed.astype(jnp.bfloat16)

    def done(i, carry):
        t = lax.rem(me + i, devices)
        partial_to(t, me).wait_send()
        stat_to(t, me).wait_send()
        return carry

    lax.fori_loop(1, devices, done, 0)
    late.wait()
    early.wait()


def per_device(
    question, block_ids, block_counts, cache_keys, cache_values, frame_query, frame_keys, frame_values, frame_reach
):
    devices = lax.axis_size("seq")
    rows = question.shape[0]
    frame_rows, width = frame_query.shape
    kv_width = cache_keys.shape[1]
    half_rows = rows * HEADS // 2
    vmem = pl.BlockSpec(memory_space=pltpu.VMEM)
    anywhere = pl.BlockSpec(memory_space=pl.ANY)
    sems = pltpu.SemaphoreType.DMA((devices,))
    bf16 = jnp.bfloat16
    return pl.pallas_call(
        functools.partial(kernel, devices),
        in_specs=[vmem, vmem, vmem, vmem] + [anywhere] * 5,
        out_specs=(vmem, anywhere),
        out_shape=(
            jax.ShapeDtypeStruct(question.shape, bf16),
            jax.ShapeDtypeStruct(frame_query.shape, bf16),
        ),
        scratch_shapes=[
            pltpu.VMEM((1, HEAD_DIM), jnp.int32),
            pltpu.VMEM((2, half_rows, HEAD_DIM), bf16),
            pltpu.VMEM((2, BLK_DEV, BLOCK, kv_width // 2), bf16),
            pltpu.VMEM((2, BLK_DEV, BLOCK, kv_width // 2), bf16),
            pltpu.VMEM((frame_rows, width), bf16),
            pltpu.VMEM((frame_rows, width), bf16),
            pltpu.VMEM((WIN + frame_rows, kv_width), bf16),
            pltpu.VMEM((WIN + frame_rows, kv_width), bf16),
            pltpu.VMEM((devices, half_rows, HEAD_DIM), bf16),
            pltpu.VMEM((devices, 1, HEAD_DIM), jnp.int32),
            pltpu.SMEM((devices, 1, HEAD_DIM), jnp.int32),
            pltpu.VMEM((devices, half_rows, HEAD_DIM), bf16),
            pltpu.VMEM((devices, 8, HEAD_DIM), jnp.float32),
            pltpu.VMEM((devices, half_rows, HEAD_DIM), bf16),
            pltpu.VMEM((devices, 8, HEAD_DIM), jnp.float32),
            pltpu.SemaphoreType.DMA((8,)),
            pltpu.SemaphoreType.DMA((4,)),
            pltpu.SemaphoreType.DMA((4,)),
            sems, sems, sems, sems, sems, sems, sems, sems,
        ],
        compiler_params=pltpu.CompilerParams(collective_id=0, has_side_effects=True),
    )(
        block_ids, block_counts.reshape(1, 1), question, frame_reach.reshape(frame_rows // WIN, WIN), cache_keys.reshape(BLK_DEV, BLOCK, kv_width),
        cache_values.reshape(BLK_DEV, BLOCK, kv_width), frame_query, frame_keys, frame_values,
    )


def solution(mesh):
    flat = P(("dp", "seq"))
    wide = P(("dp", "seq"), None)
    return jax.shard_map(
        per_device,
        mesh=mesh,
        in_specs=(wide, wide, flat, wide, wide, wide, wide, wide, flat),
        out_specs=(wide, wide),
        check_vma=False,
    )
```

```python
import functools
import math

import jax
import jax.numpy as jnp
from jax import lax
from jax.experimental import pallas as pl
from jax.experimental.pallas import tpu as pltpu
from jax.sharding import PartitionSpec as P

HEADS = 28
KV_HEADS = 4
HEAD_DIM = 128
GROUP = 7
BLOCK = 128
WIN = 128
BLK_DEV = 8
COLUMN = 8
NEGATIVE = -1e30
EXP2_SCALE = HEAD_DIM ** (-0.5) * math.log2(math.e)


def dot_t(a, b):
    return lax.dot_general(a, b, (((1,), (1,)), ((), ())), preferred_element_type=jnp.float32)


def frame_block(block, first_index, fq, fo, fk, fv, reach_ref):
    row = lax.broadcasted_iota(jnp.int32, (WIN, WIN), 0)
    col = lax.broadcasted_iota(jnp.int32, (WIN, WIN), 1)
    current = col <= row
    distance = jnp.where(current, row - col, row - col + WIN)
    reach = jnp.transpose(jnp.broadcast_to(reach_ref[block : block + 1, :], (WIN, WIN)))
    allowed = distance < reach
    if block == 0:
        allowed = allowed & (current | jnp.logical_not(first_index))
    bias = jnp.where(allowed, 0.0, NEGATIVE)
    own = jnp.where(current, 1.0, 0.0).astype(jnp.bfloat16)
    before = jnp.where(current, 0.0, 1.0).astype(jnp.bfloat16)
    ones = jnp.ones((2 * WIN, HEAD_DIM), jnp.bfloat16)
    rows = slice(block * WIN, (block + 1) * WIN)
    window = slice(block * WIN, (block + 2) * WIN)

    def step(kv, carry):
        at = pl.ds(pl.multiple_of(kv * HEAD_DIM, HEAD_DIM), HEAD_DIM)
        keys = fk[window, at]
        values = jnp.concatenate([fv[window, at], ones], 1)
        for g in range(GROUP):
            lanes = pl.ds(pl.multiple_of((kv * GROUP + g) * HEAD_DIM, HEAD_DIM), HEAD_DIM)
            both = dot_t(fq[rows, lanes], keys)
            scores = jnp.where(current, both[:, WIN:], both[:, :WIN]) + bias
            highest = jnp.max(scores, axis=1, keepdims=True)
            weights = jnp.exp2((scores - highest) * EXP2_SCALE).astype(jnp.bfloat16)
            split = jnp.concatenate([weights * before, weights * own], 1)
            mixed = jnp.dot(split, values, preferred_element_type=jnp.float32)
            fo[rows, lanes] = (mixed[:, :HEAD_DIM] / mixed[:, HEAD_DIM:]).astype(jnp.bfloat16)
        return carry

    lax.fori_loop(0, KV_HEADS, step, 0)


def tile_partial(q, keys, values, bias):
    stat = jnp.zeros((8, HEAD_DIM), jnp.float32)
    lane = lax.broadcasted_iota(jnp.int32, (8, HEAD_DIM), 1)
    rows = GROUP * 8
    head_row = lax.broadcasted_iota(jnp.int32, (2 * rows, HEAD_DIM), 0)
    upper = jnp.where(head_row < rows, 1.0, 0.0).astype(jnp.bfloat16)
    lower = jnp.where(head_row < rows, 0.0, 1.0).astype(jnp.bfloat16)
    scores = dot_t(jnp.concatenate([q * upper, q * lower], 1), keys) + bias
    highest = jnp.max(scores, axis=1, keepdims=True)
    weights = jnp.exp2((scores - highest) * EXP2_SCALE)
    total = jnp.sum(weights, axis=1, keepdims=True)
    mixed = jnp.dot(weights.astype(jnp.bfloat16), values, preferred_element_type=jnp.float32)
    for head in range(2 * GROUP):
        part = slice(head * 8, head * 8 + 8)
        stat = jnp.where(lane == head, highest[part], stat)
        stat = jnp.where(lane == head + 32, total[part], stat)
    return jnp.where(head_row < rows, mixed[:, :HEAD_DIM], mixed[:, HEAD_DIM:]).astype(jnp.bfloat16), stat


def pick_row(ids_ref, count_ref, devices):
    width = ids_ref.shape[1]
    ids = jnp.concatenate([ids_ref[...], jnp.full((1, HEAD_DIM - width), -1, jnp.int32)], 1)
    ids = jnp.transpose(jnp.broadcast_to(ids, (HEAD_DIM, HEAD_DIM)))
    slot = lax.broadcasted_iota(jnp.int32, ids.shape, 0)
    lane = lax.broadcasted_iota(jnp.int32, ids.shape, 1)
    holder = jnp.where(lane < devices, lane, lane - devices)
    held = (slot < count_ref[...]) & (ids >= 0) & ((ids >> 3) == holder)
    low = jnp.min(jnp.where(held, ids & (BLK_DEV - 1), BLK_DEV), axis=0, keepdims=True)
    high = jnp.max(jnp.where(held, ids & (BLK_DEV - 1), -1), axis=0, keepdims=True)
    return jnp.where(lane[:1] < devices, low, high)


def kernel(
    devices,
    ids_ref, count_ref, question_ref, reach_ref, ck_ref, cv_ref, fq_ref, fk_ref, fv_ref,
    a_ref, fo_ref,
    picks_ref, q_ref, kk, vv, fq, fo, fk, fv, q_all, picks_all, picks_s, ob, sb, og, sg,
    local, swap_send, swap_recv, b_send, b_recv, q_send, q_recv, p_send, p_recv, o_send, o_recv, s_send, s_recv,
):
    me = lax.axis_index("seq")
    core = lax.rem(me, 2)
    other = 1 - core
    partner = me + 1 - 2 * core
    after = lax.rem(me + 1, devices)
    half = 2 * HEAD_DIM
    rows = fq.shape[0]

    def here(src, dst, i):
        return pltpu.make_async_copy(src, dst, local.at[i])

    def there(src, dst, send, recv, device):
        return pltpu.make_async_remote_copy(
            src_ref=src, dst_ref=dst, send_sem=send, recv_sem=recv,
            device_id={"seq": device}, device_id_type=pl.DeviceIdType.MESH,
        )

    mine = pl.ds(pl.multiple_of(core * half, half), half)
    theirs = pl.ds(pl.multiple_of(other * half, half), half)
    loads = [
        here(fq_ref, fq, 0),
        here(fk_ref, fk.at[pl.ds(WIN, rows)], 1),
        here(fv_ref, fv.at[pl.ds(WIN, rows)], 2),
        here(ck_ref.at[:, :, mine], kk.at[core], 3),
        here(cv_ref.at[:, :, mine], vv.at[core], 4),
    ]
    for load in loads:
        load.start()

    barrier = pltpu.get_barrier_semaphore()

    def greet(i, carry):
        pl.semaphore_signal(
            barrier, inc=1, device_id={"seq": lax.rem(me + i, devices)}, device_id_type=pl.DeviceIdType.MESH
        )
        return carry

    lax.fori_loop(1, devices, greet, 0)
    picks_ref[...] = pick_row(ids_ref, count_ref, devices)
    for head in range(HEADS):
        at = head % (HEADS // 2) * 8
        q_ref[head // (HEADS // 2), at : at + 8, :] = question_ref[:, head * HEAD_DIM : (head + 1) * HEAD_DIM]
    pl.semaphore_wait(barrier, devices - 1)

    edges = [
        there(fk_ref.at[pl.ds(rows - WIN, WIN)], fk.at[pl.ds(0, WIN)], swap_send.at[0], swap_recv.at[0], after),
        there(fv_ref.at[pl.ds(rows - WIN, WIN)], fv.at[pl.ds(0, WIN)], swap_send.at[1], swap_recv.at[1], after),
    ]
    swaps = [
        there(ck_ref.at[:, :, theirs], kk.at[core], swap_send.at[2], swap_recv.at[2], partner),
        there(cv_ref.at[:, :, theirs], vv.at[core], swap_send.at[3], swap_recv.at[3], partner),
    ]
    swaps_in = [
        there(ck_ref.at[:, :, theirs], kk.at[other], swap_send.at[2], swap_recv.at[2], partner),
        there(cv_ref.at[:, :, theirs], vv.at[other], swap_send.at[3], swap_recv.at[3], partner),
    ]
    own = [here(q_ref.at[core], q_all.at[me], 5), here(picks_ref, picks_all.at[me], 6)]
    for copy in own:
        copy.start()

    def question_to(t, slot):
        return there(q_ref.at[lax.rem(t, 2)], q_all.at[slot], q_send.at[t], q_recv.at[slot], t)

    def picks_to(t, slot):
        return there(picks_ref, picks_all.at[slot], p_send.at[t], p_recv.at[slot], t)

    def partial_to(t, slot):
        return there(ob.at[t], og.at[slot], o_send.at[t], o_recv.at[slot], t)

    def stat_to(t, slot):
        return there(sb.at[t], sg.at[slot], s_send.at[t], s_recv.at[slot], t)

    column = me // COLUMN * COLUMN

    def in_column(i):
        return column + lax.rem(me - column + i, COLUMN)

    def columns_on(i):
        return lax.rem(column + i * COLUMN, devices)

    def block_to(first, count, steps, i):
        block = q_all.at[pl.ds(first, count)]
        return there(block, block, b_send.at[i], b_recv.at[i], lax.rem(me + steps * COLUMN, devices))

    around = devices // COLUMN - 1
    part = COLUMN // 2
    blocks_out = [block_to(column, COLUMN, 1, 0), block_to(column, COLUMN, around, 1)]
    blocks_in = [block_to(columns_on(around), COLUMN, 1, 0), block_to(columns_on(1), COLUMN, around, 1)]
    parts_out = [block_to(columns_on(around), part, 1, 2), block_to(columns_on(1) + part, part, around, 3)]
    parts_in = [block_to(columns_on(2), part, 1, 2), block_to(columns_on(2) + part, part, around, 3)]

    def send_questions(i, carry):
        question_to(in_column(i), me).start()
        return carry

    def send_picks(i, carry):
        picks_to(lax.rem(me + i, devices), me).start()
        return carry

    lax.fori_loop(1, COLUMN, send_questions, 0)
    for copy in edges:
        copy.start()
    lax.fori_loop(1, devices, send_picks, 0)
    for copy in swaps:
        copy.start()

    for load in loads[:3]:
        load.wait()
    frame_block(1, me == 0, fq, fo, fk, fv, reach_ref)

    def got_question(i, carry):
        question_to(in_column(i), in_column(i)).wait_recv()
        return carry

    lax.fori_loop(1, COLUMN, got_question, 0)
    for copy in own:
        copy.wait()
    for copy in blocks_out:
        copy.start()
    for copy in edges:
        copy.wait_recv()
    frame_block(0, me == 0, fq, fo, fk, fv, reach_ref)
    late = here(fo.at[pl.ds(WIN, WIN)], fo_ref.at[pl.ds(WIN, WIN)], 0)
    late.start()

    for load in loads[3:]:
        load.wait()

    def got_picks(i, carry):
        t = lax.rem(me + devices - i, devices)
        picks_to(t, t).wait_recv()
        return carry

    lax.fori_loop(1, devices, got_picks, 0)
    to_scalars = here(picks_all, picks_s, 7)
    to_scalars.start()
    for copy in swaps_in:
        copy.wait_recv()
    to_scalars.wait()

    chip = me - core
    block_of = lax.broadcasted_iota(jnp.int32, (1, 4 * BLOCK), 1) // BLOCK

    def gathered(t):
        keys, values = [], []
        bias = jnp.zeros((1, 4 * BLOCK), jnp.float32)
        for c in range(2):
            low = picks_s[t, 0, chip + c]
            high = picks_s[t, 0, devices + chip + c]
            usable = (low < BLK_DEV, (high >= 0) & (high != low))
            index = (jnp.minimum(low, BLK_DEV - 1), jnp.maximum(high, 0))
            for j in range(2):
                keys.append(kk[c, index[j]])
                values.append(vv[c, index[j]])
                bias = jnp.where(block_of == 2 * c + j, jnp.where(usable[j], 0.0, NEGATIVE), bias)
        return jnp.concatenate(keys, 0), jnp.concatenate(values, 0), bias

    def tile_of(j, u):
        return columns_on(j // (COLUMN // 2)) + lax.rem(me - column - core + 2 * j, COLUMN) + u

    def send_partial(t):
        partial_to(t, me).start()
        stat_to(t, me).start()

    def step(j, carry):
        @pl.when(j == COLUMN // 2)
        def _():
            for arrival, onward in zip(blocks_in, parts_out):
                arrival.wait_recv()
                onward.start()

        @pl.when(j == COLUMN)
        def _():
            for arrival in parts_in:
                arrival.wait_recv()

        results = [tile_partial(q_all[tile_of(j, u)], *gathered(tile_of(j, u))) for u in range(2)]
        for u in range(2):
            ob[tile_of(j, u)], sb[tile_of(j, u)] = results[u]

        @pl.when(j == 1)
        def _():
            send_partial(partner)

        @pl.when(j > 1)
        def _():
            for u in range(2):
                send_partial(tile_of(j - 1, u))

        return carry

    pairs = devices // 2
    lax.fori_loop(0, pairs, step, 0)
    for u in range(2):
        send_partial(tile_of(pairs - 1, u))
    keep = [here(ob.at[me], og.at[me], 1), here(sb.at[me], sg.at[me], 2)]
    for copy in keep:
        copy.start()
    early = here(fo.at[pl.ds(0, WIN)], fo_ref.at[pl.ds(0, WIN)], 3)
    early.start()

    def question_sent(i, carry):
        question_to(in_column(i), me).wait_send()
        return carry

    def picks_sent(i, carry):
        picks_to(lax.rem(me + i, devices), me).wait_send()
        return carry

    lax.fori_loop(1, COLUMN, question_sent, 0)
    lax.fori_loop(1, devices, picks_sent, 0)
    for copy in edges + swaps + blocks_out + parts_out:
        copy.wait_send()
    for copy in keep:
        copy.wait()

    def arrived(i, carry):
        t = lax.rem(me + i, devices)
        partial_to(t, t).wait_recv()
        stat_to(t, t).wait_recv()
        return carry

    lax.fori_loop(1, devices, arrived, 0)

    for h in range(2):
        stats = [sg[2 * c + h] for c in range(devices // 2)]
        highest = stats[0]
        for s in stats[1:]:
            highest = jnp.maximum(highest, s)
        scales = [jnp.exp2((s - highest) * EXP2_SCALE) for s in stats]
        total = jnp.zeros_like(highest)
        for s, scale in zip(stats, scales):
            total = total + scale * pltpu.roll(s, HEAD_DIM - 32, 1)
        shares = [scale / total for scale in scales]
        for head in range(HEADS // 2):
            mixed = jnp.zeros((8, HEAD_DIM), jnp.float32)
            for c in range(devices // 2):
                part = og[2 * c + h, head * 8 : head * 8 + 8, :].astype(jnp.float32)
                mixed = mixed + shares[c][:, head : head + 1] * part
            whole = h * (HEADS // 2) + head
            a_ref[:, whole * HEAD_DIM : (whole + 1) * HEAD_DIM] = mixed.astype(jnp.bfloat16)

    def done(i, carry):
        t = lax.rem(me + i, devices)
        partial_to(t, me).wait_send()
        stat_to(t, me).wait_send()
        return carry

    lax.fori_loop(1, devices, done, 0)
    late.wait()
    early.wait()


def per_device(
    question, block_ids, block_counts, cache_keys, cache_values, frame_query, frame_keys, frame_values, frame_reach
):
    devices = lax.axis_size("seq")
    rows = question.shape[0]
    frame_rows, width = frame_query.shape
    kv_width = cache_keys.shape[1]
    half_rows = rows * HEADS // 2
    vmem = pl.BlockSpec(memory_space=pltpu.VMEM)
    anywhere = pl.BlockSpec(memory_space=pl.ANY)
    sems = pltpu.SemaphoreType.DMA((devices,))
    bf16 = jnp.bfloat16
    return pl.pallas_call(
        functools.partial(kernel, devices),
        in_specs=[vmem, vmem, vmem, vmem] + [anywhere] * 5,
        out_specs=(vmem, anywhere),
        out_shape=(
            jax.ShapeDtypeStruct(question.shape, bf16),
            jax.ShapeDtypeStruct(frame_query.shape, bf16),
        ),
        scratch_shapes=[
            pltpu.VMEM((1, HEAD_DIM), jnp.int32),
            pltpu.VMEM((2, half_rows, HEAD_DIM), bf16),
            pltpu.VMEM((2, BLK_DEV, BLOCK, kv_width // 2), bf16),
            pltpu.VMEM((2, BLK_DEV, BLOCK, kv_width // 2), bf16),
            pltpu.VMEM((frame_rows, width), bf16),
            pltpu.VMEM((frame_rows, width), bf16),
            pltpu.VMEM((WIN + frame_rows, kv_width), bf16),
            pltpu.VMEM((WIN + frame_rows, kv_width), bf16),
            pltpu.VMEM((devices, half_rows, HEAD_DIM), bf16),
            pltpu.VMEM((devices, 1, HEAD_DIM), jnp.int32),
            pltpu.SMEM((devices, 1, HEAD_DIM), jnp.int32),
            pltpu.VMEM((devices, half_rows, HEAD_DIM), bf16),
            pltpu.VMEM((devices, 8, HEAD_DIM), jnp.float32),
            pltpu.VMEM((devices, half_rows, HEAD_DIM), bf16),
            pltpu.VMEM((devices, 8, HEAD_DIM), jnp.float32),
            pltpu.SemaphoreType.DMA((8,)),
            pltpu.SemaphoreType.DMA((4,)),
            pltpu.SemaphoreType.DMA((4,)),
            pltpu.SemaphoreType.DMA((4,)),
            pltpu.SemaphoreType.DMA((4,)),
            sems, sems, sems, sems, sems, sems, sems, sems,
        ],
        compiler_params=pltpu.CompilerParams(collective_id=0, has_side_effects=True),
    )(
        block_ids, block_counts.reshape(1, 1), question, frame_reach.reshape(frame_rows // WIN, WIN), cache_keys.reshape(BLK_DEV, BLOCK, kv_width),
        cache_values.reshape(BLK_DEV, BLOCK, kv_width), frame_query, frame_keys, frame_values,
    )


def solution(mesh):
    flat = P(("dp", "seq"))
    wide = P(("dp", "seq"), None)
    return jax.shard_map(
        per_device,
        mesh=mesh,
        in_specs=(wide, wide, flat, wide, wide, wide, wide, wide, flat),
        out_specs=(wide, wide),
        check_vma=False,
    )
```

```python
import functools
import math

import jax
import jax.numpy as jnp
from jax import lax
from jax.experimental import pallas as pl
from jax.experimental.pallas import tpu as pltpu
from jax.sharding import PartitionSpec as P

HEADS = 28
KV_HEADS = 4
HEAD_DIM = 128
GROUP = 7
BLOCK = 128
WIN = 128
BLK_DEV = 8
COLUMN = 8
NEGATIVE = -1e30
EXP2_SCALE = HEAD_DIM ** (-0.5) * math.log2(math.e)


def dot_t(a, b):
    return lax.dot_general(a, b, (((1,), (1,)), ((), ())), preferred_element_type=jnp.float32)


def frame_block(block, first_index, fq, fo, fk, fv, reach_ref):
    row = lax.broadcasted_iota(jnp.int32, (WIN, WIN), 0)
    col = lax.broadcasted_iota(jnp.int32, (WIN, WIN), 1)
    current = col <= row
    distance = jnp.where(current, row - col, row - col + WIN)
    reach = jnp.transpose(jnp.broadcast_to(reach_ref[block : block + 1, :], (WIN, WIN)))
    allowed = distance < reach
    if block == 0:
        allowed = allowed & (current | jnp.logical_not(first_index))
    bias = jnp.where(allowed, 0.0, NEGATIVE)
    own = jnp.where(current, 1.0, 0.0).astype(jnp.bfloat16)
    before = jnp.where(current, 0.0, 1.0).astype(jnp.bfloat16)
    ones = jnp.ones((2 * WIN, HEAD_DIM), jnp.bfloat16)
    rows = slice(block * WIN, (block + 1) * WIN)
    window = slice(block * WIN, (block + 2) * WIN)

    def step(kv, carry):
        at = pl.ds(pl.multiple_of(kv * HEAD_DIM, HEAD_DIM), HEAD_DIM)
        keys = fk[window, at]
        values = jnp.concatenate([fv[window, at], ones], 1)
        for g in range(GROUP):
            lanes = pl.ds(pl.multiple_of((kv * GROUP + g) * HEAD_DIM, HEAD_DIM), HEAD_DIM)
            both = dot_t(fq[rows, lanes], keys)
            scores = jnp.where(current, both[:, WIN:], both[:, :WIN]) + bias
            highest = jnp.max(scores, axis=1, keepdims=True)
            weights = jnp.exp2((scores - highest) * EXP2_SCALE).astype(jnp.bfloat16)
            split = jnp.concatenate([weights * before, weights * own], 1)
            mixed = jnp.dot(split, values, preferred_element_type=jnp.float32)
            fo[rows, lanes] = (mixed[:, :HEAD_DIM] / mixed[:, HEAD_DIM:]).astype(jnp.bfloat16)
        return carry

    lax.fori_loop(0, KV_HEADS, step, 0)


def tile_partial(q, keys, values, bias):
    stat = jnp.zeros((8, HEAD_DIM), jnp.float32)
    lane = lax.broadcasted_iota(jnp.int32, (8, HEAD_DIM), 1)
    rows = GROUP * 8
    head_row = lax.broadcasted_iota(jnp.int32, (2 * rows, HEAD_DIM), 0)
    upper = jnp.where(head_row < rows, 1.0, 0.0).astype(jnp.bfloat16)
    lower = jnp.where(head_row < rows, 0.0, 1.0).astype(jnp.bfloat16)
    scores = dot_t(jnp.concatenate([q * upper, q * lower], 1), keys) + bias
    highest = jnp.max(scores, axis=1, keepdims=True)
    weights = jnp.exp2((scores - highest) * EXP2_SCALE)
    total = jnp.sum(weights, axis=1, keepdims=True)
    mixed = jnp.dot(weights.astype(jnp.bfloat16), values, preferred_element_type=jnp.float32)
    for head in range(2 * GROUP):
        part = slice(head * 8, head * 8 + 8)
        stat = jnp.where(lane == head, highest[part], stat)
        stat = jnp.where(lane == head + 32, total[part], stat)
    return jnp.where(head_row < rows, mixed[:, :HEAD_DIM], mixed[:, HEAD_DIM:]).astype(jnp.bfloat16), stat


def pick_row(ids_ref, count_ref, devices):
    width = ids_ref.shape[1]
    ids = jnp.concatenate([ids_ref[...], jnp.full((1, HEAD_DIM - width), -1, jnp.int32)], 1)
    ids = jnp.transpose(jnp.broadcast_to(ids, (HEAD_DIM, HEAD_DIM)))
    slot = lax.broadcasted_iota(jnp.int32, ids.shape, 0)
    lane = lax.broadcasted_iota(jnp.int32, ids.shape, 1)
    holder = jnp.where(lane < devices, lane, lane - devices)
    held = (slot < count_ref[...]) & (ids >= 0) & ((ids >> 3) == holder)
    low = jnp.min(jnp.where(held, ids & (BLK_DEV - 1), BLK_DEV), axis=0, keepdims=True)
    high = jnp.max(jnp.where(held, ids & (BLK_DEV - 1), -1), axis=0, keepdims=True)
    return jnp.where(lane[:1] < devices, low, high)


def kernel(
    devices,
    ids_ref, count_ref, question_ref, reach_ref, ck_ref, cv_ref, fq_ref, fk_ref, fv_ref,
    fo_ref, og, sg,
    picks_ref, q_ref, kk, vv, fq, fo, fk, fv, q_all, picks_all, picks_s, ob, sb,
    local, swap_send, swap_recv, b_send, b_recv, q_send, q_recv, p_send, p_recv, o_send, o_recv, s_send, s_recv,
):
    me = lax.axis_index("seq")
    core = lax.rem(me, 2)
    other = 1 - core
    partner = me + 1 - 2 * core
    after = lax.rem(me + 1, devices)
    half = 2 * HEAD_DIM
    rows = fq.shape[0]

    def here(src, dst, i):
        return pltpu.make_async_copy(src, dst, local.at[i])

    def there(src, dst, send, recv, device):
        return pltpu.make_async_remote_copy(
            src_ref=src, dst_ref=dst, send_sem=send, recv_sem=recv,
            device_id={"seq": device}, device_id_type=pl.DeviceIdType.MESH,
        )

    mine = pl.ds(pl.multiple_of(core * half, half), half)
    theirs = pl.ds(pl.multiple_of(other * half, half), half)
    loads = [
        here(fq_ref, fq, 0),
        here(fk_ref, fk.at[pl.ds(WIN, rows)], 1),
        here(fv_ref, fv.at[pl.ds(WIN, rows)], 2),
        here(ck_ref.at[:, :, mine], kk.at[core], 3),
        here(cv_ref.at[:, :, mine], vv.at[core], 4),
    ]
    for load in loads:
        load.start()

    barrier = pltpu.get_barrier_semaphore()

    def greet(i, carry):
        pl.semaphore_signal(
            barrier, inc=1, device_id={"seq": lax.rem(me + i, devices)}, device_id_type=pl.DeviceIdType.MESH
        )
        return carry

    lax.fori_loop(1, devices, greet, 0)
    picks_ref[...] = pick_row(ids_ref, count_ref, devices)
    for head in range(HEADS):
        at = head % (HEADS // 2) * 8
        q_ref[head // (HEADS // 2), at : at + 8, :] = question_ref[:, head * HEAD_DIM : (head + 1) * HEAD_DIM]
    pl.semaphore_wait(barrier, devices - 1)

    edges = [
        there(fk_ref.at[pl.ds(rows - WIN, WIN)], fk.at[pl.ds(0, WIN)], swap_send.at[0], swap_recv.at[0], after),
        there(fv_ref.at[pl.ds(rows - WIN, WIN)], fv.at[pl.ds(0, WIN)], swap_send.at[1], swap_recv.at[1], after),
    ]
    swaps = [
        there(ck_ref.at[:, :, theirs], kk.at[core], swap_send.at[2], swap_recv.at[2], partner),
        there(cv_ref.at[:, :, theirs], vv.at[core], swap_send.at[3], swap_recv.at[3], partner),
    ]
    swaps_in = [
        there(ck_ref.at[:, :, theirs], kk.at[other], swap_send.at[2], swap_recv.at[2], partner),
        there(cv_ref.at[:, :, theirs], vv.at[other], swap_send.at[3], swap_recv.at[3], partner),
    ]
    own = [here(q_ref.at[core], q_all.at[me], 5), here(picks_ref, picks_all.at[me], 6)]
    for copy in own:
        copy.start()

    def question_to(t, slot):
        return there(q_ref.at[lax.rem(t, 2)], q_all.at[slot], q_send.at[t], q_recv.at[slot], t)

    def picks_to(t, slot):
        return there(picks_ref, picks_all.at[slot], p_send.at[t], p_recv.at[slot], t)

    def partial_to(t, slot):
        return there(ob.at[t], og.at[slot], o_send.at[t], o_recv.at[slot], t)

    def stat_to(t, slot):
        return there(sb.at[t], sg.at[slot], s_send.at[t], s_recv.at[slot], t)

    column = me // COLUMN * COLUMN

    def in_column(i):
        return column + lax.rem(me - column + i, COLUMN)

    def columns_on(i):
        return lax.rem(column + i * COLUMN, devices)

    def block_to(first, count, steps, i):
        block = q_all.at[pl.ds(first, count)]
        return there(block, block, b_send.at[i], b_recv.at[i], lax.rem(me + steps * COLUMN, devices))

    around = devices // COLUMN - 1
    part = COLUMN // 2
    blocks_out = [block_to(column, COLUMN, 1, 0), block_to(column, COLUMN, around, 1)]
    blocks_in = [block_to(columns_on(around), COLUMN, 1, 0), block_to(columns_on(1), COLUMN, around, 1)]
    parts_out = [block_to(columns_on(around), part, 1, 2), block_to(columns_on(1) + part, part, around, 3)]
    parts_in = [block_to(columns_on(2), part, 1, 2), block_to(columns_on(2) + part, part, around, 3)]

    def send_questions(i, carry):
        question_to(in_column(i), me).start()
        return carry

    def send_picks(i, carry):
        picks_to(lax.rem(me + i, devices), me).start()
        return carry

    lax.fori_loop(1, COLUMN, send_questions, 0)
    for copy in edges:
        copy.start()
    lax.fori_loop(1, devices, send_picks, 0)
    for copy in swaps:
        copy.start()

    for load in loads[:3]:
        load.wait()
    frame_block(1, me == 0, fq, fo, fk, fv, reach_ref)

    def got_question(i, carry):
        question_to(in_column(i), in_column(i)).wait_recv()
        return carry

    lax.fori_loop(1, COLUMN, got_question, 0)
    for copy in own:
        copy.wait()
    for copy in blocks_out:
        copy.start()
    for copy in edges:
        copy.wait_recv()
    frame_block(0, me == 0, fq, fo, fk, fv, reach_ref)
    late = here(fo.at[pl.ds(WIN, WIN)], fo_ref.at[pl.ds(WIN, WIN)], 0)
    late.start()

    for load in loads[3:]:
        load.wait()

    def got_picks(i, carry):
        t = lax.rem(me + devices - i, devices)
        picks_to(t, t).wait_recv()
        return carry

    lax.fori_loop(1, devices, got_picks, 0)
    to_scalars = here(picks_all, picks_s, 7)
    to_scalars.start()
    for copy in swaps_in:
        copy.wait_recv()
    to_scalars.wait()

    chip = me - core
    block_of = lax.broadcasted_iota(jnp.int32, (1, 4 * BLOCK), 1) // BLOCK

    def gathered(t):
        keys, values = [], []
        bias = jnp.zeros((1, 4 * BLOCK), jnp.float32)
        for c in range(2):
            low = picks_s[t, 0, chip + c]
            high = picks_s[t, 0, devices + chip + c]
            usable = (low < BLK_DEV, (high >= 0) & (high != low))
            index = (jnp.minimum(low, BLK_DEV - 1), jnp.maximum(high, 0))
            for j in range(2):
                keys.append(kk[c, index[j]])
                values.append(vv[c, index[j]])
                bias = jnp.where(block_of == 2 * c + j, jnp.where(usable[j], 0.0, NEGATIVE), bias)
        return jnp.concatenate(keys, 0), jnp.concatenate(values, 0), bias

    def tile_of(j, u):
        return columns_on(j // (COLUMN // 2)) + lax.rem(me - column - core + 2 * j, COLUMN) + u

    def send_partial(t):
        partial_to(t, me).start()
        stat_to(t, me).start()

    def step(j, carry):
        @pl.when(j == COLUMN // 2)
        def _():
            for arrival, onward in zip(blocks_in, parts_out):
                arrival.wait_recv()
                onward.start()

        @pl.when(j == COLUMN)
        def _():
            for arrival in parts_in:
                arrival.wait_recv()

        results = [tile_partial(q_all[tile_of(j, u)], *gathered(tile_of(j, u))) for u in range(2)]
        for u in range(2):
            ob[tile_of(j, u)], sb[tile_of(j, u)] = results[u]

        @pl.when(j == 1)
        def _():
            send_partial(partner)

        @pl.when(j > 1)
        def _():
            for u in range(2):
                send_partial(tile_of(j - 1, u))

        return carry

    pairs = devices // 2
    lax.fori_loop(0, pairs, step, 0)
    for u in range(2):
        send_partial(tile_of(pairs - 1, u))
    keep = [here(ob.at[me], og.at[me], 1), here(sb.at[me], sg.at[me], 2)]
    for copy in keep:
        copy.start()
    early = here(fo.at[pl.ds(0, WIN)], fo_ref.at[pl.ds(0, WIN)], 3)
    early.start()

    def question_sent(i, carry):
        question_to(in_column(i), me).wait_send()
        return carry

    def picks_sent(i, carry):
        picks_to(lax.rem(me + i, devices), me).wait_send()
        return carry

    lax.fori_loop(1, COLUMN, question_sent, 0)
    lax.fori_loop(1, devices, picks_sent, 0)
    for copy in edges + swaps + blocks_out + parts_out:
        copy.wait_send()
    for copy in keep:
        copy.wait()

    def arrived(i, carry):
        t = lax.rem(me + i, devices)
        partial_to(t, t).wait_recv()
        stat_to(t, t).wait_recv()
        return carry

    lax.fori_loop(1, devices, arrived, 0)

    def done(i, carry):
        t = lax.rem(me + i, devices)
        partial_to(t, me).wait_send()
        stat_to(t, me).wait_send()
        return carry

    lax.fori_loop(1, devices, done, 0)
    late.wait()
    early.wait()


def finish_kernel(og, sg, frame_ref, a_ref, fo_ref):
    fo_ref[...] = frame_ref[...]

    @pl.when(pl.program_id(0) == 0)
    def _():
        combine(og, sg, a_ref)


def combine(og, sg, a_ref):
    devices = og.shape[0]
    for h in range(2):
        stats = [sg[2 * c + h] for c in range(devices // 2)]
        highest = stats[0]
        for s in stats[1:]:
            highest = jnp.maximum(highest, s)
        scales = [jnp.exp2((s - highest) * EXP2_SCALE) for s in stats]
        total = jnp.zeros_like(highest)
        for s, scale in zip(stats, scales):
            total = total + scale * pltpu.roll(s, HEAD_DIM - 32, 1)
        shares = [scale / total for scale in scales]
        for head in range(HEADS // 2):
            mixed = jnp.zeros((8, HEAD_DIM), jnp.float32)
            for c in range(devices // 2):
                part = og[2 * c + h, head * 8 : head * 8 + 8, :].astype(jnp.float32)
                mixed = mixed + shares[c][:, head : head + 1] * part
            whole = h * (HEADS // 2) + head
            a_ref[:, whole * HEAD_DIM : (whole + 1) * HEAD_DIM] = mixed.astype(jnp.bfloat16)


def per_device(
    question, block_ids, block_counts, cache_keys, cache_values, frame_query, frame_keys, frame_values, frame_reach
):
    devices = lax.axis_size("seq")
    rows = question.shape[0]
    frame_rows, width = frame_query.shape
    kv_width = cache_keys.shape[1]
    half_rows = rows * HEADS // 2
    vmem = pl.BlockSpec(memory_space=pltpu.VMEM)
    anywhere = pl.BlockSpec(memory_space=pl.ANY)
    sems = pltpu.SemaphoreType.DMA((devices,))
    bf16 = jnp.bfloat16
    frame_out, partials, stats = pl.pallas_call(
        functools.partial(kernel, devices),
        in_specs=[vmem, vmem, vmem, vmem] + [anywhere] * 5,
        out_specs=(anywhere, anywhere, anywhere),
        out_shape=(
            jax.ShapeDtypeStruct(frame_query.shape, bf16),
            jax.ShapeDtypeStruct((devices, half_rows, HEAD_DIM), bf16),
            jax.ShapeDtypeStruct((devices, 8, HEAD_DIM), jnp.float32),
        ),
        scratch_shapes=[
            pltpu.VMEM((1, HEAD_DIM), jnp.int32),
            pltpu.VMEM((2, half_rows, HEAD_DIM), bf16),
            pltpu.VMEM((2, BLK_DEV, BLOCK, kv_width // 2), bf16),
            pltpu.VMEM((2, BLK_DEV, BLOCK, kv_width // 2), bf16),
            pltpu.VMEM((frame_rows, width), bf16),
            pltpu.VMEM((frame_rows, width), bf16),
            pltpu.VMEM((WIN + frame_rows, kv_width), bf16),
            pltpu.VMEM((WIN + frame_rows, kv_width), bf16),
            pltpu.VMEM((devices, half_rows, HEAD_DIM), bf16),
            pltpu.VMEM((devices, 1, HEAD_DIM), jnp.int32),
            pltpu.SMEM((devices, 1, HEAD_DIM), jnp.int32),
            pltpu.VMEM((devices, half_rows, HEAD_DIM), bf16),
            pltpu.VMEM((devices, 8, HEAD_DIM), jnp.float32),
            pltpu.SemaphoreType.DMA((8,)),
            pltpu.SemaphoreType.DMA((4,)),
            pltpu.SemaphoreType.DMA((4,)),
            pltpu.SemaphoreType.DMA((4,)),
            pltpu.SemaphoreType.DMA((4,)),
            sems, sems, sems, sems, sems, sems, sems, sems,
        ],
        compiler_params=pltpu.CompilerParams(collective_id=0, has_side_effects=True),
    )(
        block_ids, block_counts.reshape(1, 1), question, frame_reach.reshape(frame_rows // WIN, WIN), cache_keys.reshape(BLK_DEV, BLOCK, kv_width),
        cache_values.reshape(BLK_DEV, BLOCK, kv_width), frame_query, frame_keys, frame_values,
    )
    steps = 4
    passed = pl.BlockSpec((frame_rows // steps, width), lambda i: (i, 0))
    return pl.pallas_call(
        finish_kernel,
        grid=(steps,),
        in_specs=[
            pl.BlockSpec(partials.shape, lambda i: (0, 0, 0)),
            pl.BlockSpec(stats.shape, lambda i: (0, 0, 0)),
            passed,
        ],
        out_specs=(pl.BlockSpec(question.shape, lambda i: (0, 0)), passed),
        out_shape=(
            jax.ShapeDtypeStruct(question.shape, bf16),
            jax.ShapeDtypeStruct(frame_query.shape, bf16),
        ),
    )(partials, stats, frame_out)


def solution(mesh):
    flat = P(("dp", "seq"))
    wide = P(("dp", "seq"), None)
    return jax.shard_map(
        per_device,
        mesh=mesh,
        in_specs=(wide, wide, flat, wide, wide, wide, wide, wide, flat),
        out_specs=(wide, wide),
        check_vma=False,
    )
```
